512 devices in a mesh: row: 32 (over y, x, core), col: 16 (over z).
Axes of the slice: x: 4, y: 4, z: 16, core: 2. Of those that a mesh axis runs over, the one named last changes fastest.
Arguments:
- covariance: bfloat16 [16384, 16384], P('row', 'col'), as said below
- coef_index: int32 [3, 16384], replicated, may hold values from 0 to 127, as said below
Outputs:
- grid_cov: float32 [4608, 4608], P('row', 'col')
The draws below stay inside these ranges and needn't reach their ends.
Inputs may be any that keep to these rules, and one draw needn't show every extreme that they name: `coef_index`: every (degree l, order m, parity c) with m <= l < 128, c in 0 and 1, and c = 0 where m = 0, names exactly one row. The rows of each order are consecutive: cosine terms by rising degree, then sine terms by rising degree. Orders m and 128 - m (0 and 64) stand next to each other, the smaller first, and fill 2 * 128 rows together; pairs start at multiples of 256. Columns follow the same index. `covariance`: Symmetric.
All inputs are finite; a program needn't handle non-finite values.
Results may differ from the reference program's by a relative error of at most 0.0028.
Values sent between devices are 32-bit elements; how exact they have to be, the bound alone decides.
A program may use at most 64 MiB of HBM per device.

```python
import math
import jax
import jax.numpy as jnp
from jax import lax

LL = 128
NLON = 384
NLAT = 12
K = 16384
NPTS = 4608


def draw_covariance(key, part):
    key_scale = jax.random.fold_in(key, 11)
    key_diag = jax.random.fold_in(key, 12)
    key_noise = jax.random.fold_in(key, 13)
    scales = jnp.exp(jax.random.uniform(key_scale, (K,), jnp.float32, 0.0, math.log(10.0)))
    diag_vals = jax.random.uniform(key_diag, (K,), jnp.float32, 0.5, 1.5)
    block_width = min(1024, K)
    nblocks = K // block_width

    def one_row(row_block):

        def one_tile(col_block):
            lower = jnp.minimum(row_block, col_block)
            upper = jnp.maximum(row_block, col_block)
            tile_key = jax.random.fold_in(key_noise, lower * nblocks + upper)
            noise = jax.random.normal(tile_key, (block_width, block_width), jnp.float32)
            flipped = jnp.where(row_block > col_block, noise.T, noise)
            return jnp.where(row_block == col_block, (noise + noise.T) * 0.70710678, flipped)
        tiles = jax.vmap(one_tile)(jnp.arange(nblocks, dtype=jnp.int32))
        tiles = jnp.transpose(tiles, (1, 0, 2)).reshape(block_width, K)
        row_scale = lax.dynamic_slice_in_dim(scales, row_block * block_width, block_width)
        row_diag = lax.dynamic_slice_in_dim(diag_vals, row_block * block_width, block_width)
        on_diag = (row_block * block_width + jnp.arange(block_width, dtype=jnp.int32))[:, None] == jnp.arange(K, dtype=jnp.int32)[None, :]
        entry = row_scale[:, None] * scales[None, :] * (0.5 * tiles + jnp.where(on_diag, row_diag[:, None], 0.0)) / (8.0 * K)
        return entry.astype(jnp.bfloat16)
    rows_out = lax.map(one_row, jnp.arange(nblocks, dtype=jnp.int32))
    return rows_out.reshape(K, K)


def draw_coef_index(key, part):
    pair_order = jax.random.permutation(jax.random.fold_in(key, 21), LL // 2).astype(jnp.int32)
    row_ids = jnp.arange(K, dtype=jnp.int32)
    pair_slot = row_ids // (2 * LL)
    offset = row_ids % (2 * LL)
    pair_ids = pair_order[pair_slot]
    first_order = pair_ids
    second_order = jnp.where(pair_ids == 0, LL // 2, LL - pair_ids)
    first_size = jnp.where(pair_ids == 0, LL, 2 * (LL - pair_ids))
    in_first = offset < first_size
    order_ids = jnp.where(in_first, first_order, second_order)
    within = jnp.where(in_first, offset, offset - first_size)
    order_len = LL - order_ids
    parity = jnp.where(order_ids == 0, 0, (within >= order_len).astype(jnp.int32))
    degree = order_ids + within - parity * order_len
    return jnp.stack([degree, order_ids, parity]).astype(jnp.int32)


def setup_inputs(seed: int = 0) -> dict:
    splits = jax.random.split(jax.random.key(seed), 3)
    return {
        "covariance": draw_covariance(jax.random.fold_in(splits[2], 71), 0),
        "coef_index": draw_coef_index(jax.random.fold_in(splits[2], 71), 0),
    }


def legendre_rows(lat_count, lon_count, degree_count):
    grid_rows = lon_count // 2
    first_row = grid_rows // 2 - lat_count // 2
    colatitude = (first_row + jnp.arange(lat_count, dtype=jnp.float32) + 0.5) * (math.pi / grid_rows)
    cosine = jnp.cos(colatitude)[:, None]
    sine_vals = jnp.sin(colatitude)[:, None]
    orders = jnp.arange(degree_count, dtype=jnp.float32)[None, :]
    growth = jnp.sqrt((2.0 * orders + 1.0) / jnp.maximum(2.0 * orders, 1.0))
    growth = jnp.where(orders == 1.0, jnp.sqrt(jnp.float32(3.0)), jnp.where(orders == 0.0, 1.0, growth))
    sectoral = jnp.exp(jnp.cumsum(jnp.log(growth), axis=1) + orders * jnp.log(sine_vals))

    def advance(state_pair, degree):
        before, earlier = state_pair
        deg_sum = degree + orders
        deg_diff = degree - orders
        alpha_lm = jnp.sqrt(jnp.maximum((2.0 * degree - 1.0) * (2.0 * degree + 1.0), 0.0) / jnp.maximum(deg_diff * deg_sum, 1.0))
        beta_lm = jnp.sqrt(jnp.maximum((2.0 * degree + 1.0) * (deg_sum - 1.0) * (deg_diff - 1.0), 0.0) / jnp.maximum(deg_diff * deg_sum * (2.0 * degree - 3.0), 1.0))
        general = alpha_lm * cosine * before - beta_lm * earlier
        current = jnp.where(orders < degree, general, jnp.where(orders == degree, sectoral, 0.0))
        return ((current, before), current)
    start_pair = (jnp.zeros((lat_count, degree_count), jnp.float32), jnp.zeros((lat_count, degree_count), jnp.float32))
    _, stacked = lax.scan(advance, start_pair, jnp.arange(degree_count, dtype=jnp.float32), unroll=16)
    return jnp.transpose(stacked, (1, 0, 2)).reshape(lat_count, degree_count * degree_count)

def fourier(modes, parity, longitudes):
    phases = longitudes[:, None] * modes[None, :] % NLON
    angles = phases.astype(jnp.float32) * (2.0 * math.pi / NLON)
    return jnp.where(parity[None, :] == 0, jnp.cos(angles), jnp.sin(angles))

def reference(covariance, coef_index):
    degree = coef_index[0]
    orders = coef_index[1]
    parity = coef_index[2]
    plm_table = legendre_rows(NLAT, NLON, LL)
    values = plm_table[:, degree * LL + orders]
    rounded = lax.optimization_barrier(values.astype(jnp.bfloat16)).astype(jnp.float32)
    rounded_t = rounded.T
    key_ids = 2 * orders + parity
    block_width = min(512, K)
    blocks = K // block_width

    def row_side(block_index):
        column_block = lax.dynamic_slice_in_dim(covariance, block_index * block_width, block_width, 1).astype(jnp.float32)
        product = rounded_t[:, :, None] * column_block[:, None, :]
        return jax.ops.segment_sum(product, key_ids, num_segments=2 * LL)
    row_pass = lax.map(row_side, jnp.arange(blocks, dtype=jnp.int32))
    row_pass_t = jnp.transpose(row_pass, (0, 3, 1, 2)).reshape(K, 2 * LL * NLAT)

    def col_side(latitude):
        weights = lax.dynamic_index_in_dim(values, latitude, 0, keepdims=False)
        return jax.ops.segment_sum(row_pass_t * weights[:, None], key_ids, num_segments=2 * LL)
    second = lax.map(col_side, jnp.arange(NLAT, dtype=jnp.int32))
    second = second.reshape(NLAT, 2 * LL, 2 * LL, NLAT)
    mode_ids = jnp.arange(2 * LL, dtype=jnp.int32)
    dft_table = fourier(mode_ids // 2, mode_ids % 2, jnp.arange(NLON, dtype=jnp.int32))
    half_done = jnp.einsum('akbi,jb->akji', second, dft_table, precision=lax.Precision.HIGHEST)
    grid_cov = jnp.einsum('akji,Jk->jiJa', half_done, dft_table, precision=lax.Precision.HIGHEST)
    return grid_cov.reshape(NPTS, NPTS)
```

```python
import math

import jax
import jax.numpy as jnp
from jax import lax
from jax.experimental import pallas as pl
from jax.experimental.pallas import tpu as pltpu
from jax.sharding import PartitionSpec as P

LL = 128
NLON = 384
NLAT = 12
F32 = jnp.float32
BF16 = jnp.bfloat16
I32 = jnp.int32
MESH = pl.DeviceIdType.MESH

NROW = 32
NCOL = 16
ZW = 9
RW = 27
LANES = 384


def iota(shape, dim):
    return lax.broadcasted_iota(I32, shape, dim)


def split(x):
    hi = x.astype(BF16)
    return hi, (x - hi.astype(F32)).astype(BF16)


def mm(a, b, dims=((1,), (0,))):
    return lax.dot_general(a, b, (dims, ((), ())), preferred_element_type=F32)


def key_orders(pair, second, firsts):
    n = pair.shape[1]
    hit = iota((64, n), 0) == pair
    first = jnp.sum(jnp.where(hit, firsts, 0.0), axis=0, keepdims=True)
    other = jnp.where(first == 0.0, 64.0, 128.0 - first)
    return jnp.where(second == 0, first, other)


def fourier(j, m, parity):
    x = j * m + (NLON - (NLON // 4) * parity)
    p = x - NLON * jnp.floor(x * (1.0 / NLON))
    s = jnp.abs(p - NLON / 2) - NLON / 4
    t = s * (2.0 * math.pi / NLON)
    t2 = t * t
    r = -1.0 / 39916800.0
    for c in (1.0 / 362880.0, -1.0 / 5040.0, 1.0 / 120.0, -1.0 / 6.0, 1.0):
        r = r * t2 + c
    return r * t


def kernel(
    cov_hbm,
    coef_hbm,
    out,
    cov,
    coef,
    firsts,
    ta,
    tb,
    ts,
    tp,
    fz_hi,
    fz_lo,
    fr_hi,
    fr_lo,
    perm,
    c_send,
    c_recv,
    d_send,
    d_recv,
    a_send,
    a_recv,
    b_send,
    b_recv,
    oa,
    ob,
    oc,
    local_sem,
    ssem,
    rsem,
):
    r = lax.axis_index("row")
    c = lax.axis_index("col")
    zw = (ZW * c + NCOL - 1) // NCOL
    z_works = (NCOL * zw) // ZW == c
    rw = (RW * r + NROW - 1) // NROW
    r_works = (NROW * rw) // RW == r

    coef_copy = pltpu.make_async_copy(coef_hbm, coef, local_sem.at[0])
    coef_copy.start()
    cov_copy = pltpu.make_async_copy(cov_hbm, cov, local_sem.at[1])
    cov_copy.start()

    barrier = pltpu.get_barrier_semaphore()

    def greet_col(k, carry):
        pl.semaphore_signal(
            barrier, inc=1, device_id={"col": lax.rem(c + k, NCOL)}, device_id_type=MESH
        )
        return carry

    def greet_row(k, carry):
        pl.semaphore_signal(
            barrier, inc=1, device_id={"row": lax.rem(r + k, NROW)}, device_id_type=MESH
        )
        return carry

    lax.fori_loop(1, NCOL, greet_col, 0)
    lax.fori_loop(1, NROW, greet_row, 0)

    coef_copy.wait()
    for p in range(64):
        firsts[p : p + 1, :] = coef[1:2, 256 * p : 256 * p + 128].astype(F32)
    first_col = firsts[...][:, 0:1]

    lane = iota((1, LANES), 1)
    on_row = lane < 128
    y = lane - 128
    lat = jnp.where(on_row, lane // 8, y // 16)
    key = jnp.where(on_row, lane % 8, y % 16)
    pair = jnp.where(on_row, 2 * r, 4 * c) + key // 4
    m = key_orders(pair, (key // 2) % 2, first_col)
    delta = (lat.astype(F32) - 5.5) * (math.pi / 192)
    d2 = delta * delta
    cos_t = -delta * (1.0 - d2 * (1.0 / 6.0) * (1.0 - d2 * (1.0 / 20.0) * (1.0 - d2 * (1.0 / 42.0))))
    sin_t = 1.0 - d2 * 0.5 * (1.0 - d2 * (1.0 / 12.0) * (1.0 - d2 * (1.0 / 30.0)))
    deg = iota((LL, LANES), 0).astype(F32)
    diff = deg - m
    total = deg + m
    above = diff > 0.0
    inv = 1.0 / jnp.maximum(diff * total, 1.0)
    a = jnp.sqrt(jnp.maximum((2.0 * deg - 1.0) * (2.0 * deg + 1.0), 0.0) * inv)
    b = jnp.sqrt(
        jnp.maximum((2.0 * deg + 1.0) * (total - 1.0) * (diff - 1.0), 0.0)
        * inv
        / jnp.maximum(2.0 * deg - 3.0, 1.0)
    )
    ta[...] = jnp.where(above, a * cos_t, 0.0)
    tb[...] = jnp.where(above, b, 0.0)
    growth = jnp.sqrt((2.0 * deg + 1.0) / jnp.maximum(2.0 * deg, 1.0))
    growth = jnp.where(deg == 1.0, math.sqrt(3.0), growth)
    ts[...] = jnp.where(deg == 0.0, 1.0, growth * sin_t)

    def advance(block, state):
        before, earlier, sect = state
        base = pl.multiple_of(block * 8, 8)
        av, bv, sv = (t[pl.ds(base, 8), :] for t in (ta, tb, ts))
        rows = []
        for s in range(8):
            sect = sect * sv[s : s + 1]
            here = (block * 8 + s).astype(F32)
            now = jnp.where(m == here, sect, av[s : s + 1] * before - bv[s : s + 1] * earlier)
            rows.append(now)
            before, earlier = now, before
        tp[pl.ds(base, 8), :] = jnp.concatenate(rows, axis=0)
        return before, earlier, sect

    zero = jnp.zeros((1, LANES), F32)
    lax.fori_loop(0, LL // 8, advance, (zero, zero, zero + 1.0))

    table = tp[...].T
    keys = (2.0 * jnp.broadcast_to(m, (LL, LANES)) + (key % 2).astype(F32)).T[:, 0:1]

    def places(row, n, at):
        return coef[row : row + 1, pl.ds(pl.multiple_of(at, 512), n)]

    row_at, col_at = 512 * r, 1024 * c
    pick = jnp.where(iota((LL, 512), 0) == places(0, 512, row_at), 1.0, 0.0).astype(BF16)
    row_keys = (2 * places(1, 512, row_at) + places(2, 512, row_at)).astype(F32)
    w_row = mm(table[0:96].astype(BF16), pick)
    w_row = jnp.where(keys[0:96] == row_keys, w_row, 0.0).astype(BF16)

    pick = jnp.where(iota((LL, 1024), 0) == places(0, 1024, col_at), 1.0, 0.0).astype(BF16)
    col_keys = (2 * places(1, 1024, col_at) + places(2, 1024, col_at)).astype(F32)
    hit = keys[128:320] == col_keys
    t_hi, t_lo = split(table[128:320])
    w_hi = jnp.where(hit, mm(t_hi, pick), 0.0).astype(BF16)
    w_lo = jnp.where(hit, mm(t_lo, pick), 0.0).astype(BF16)

    cov_copy.wait()
    f_hi, f_lo = split(mm(w_row, cov[...]))
    last = ((1,), (1,))
    spec = mm(w_hi, f_hi, last) + mm(w_lo, f_hi, last) + mm(w_hi, f_lo, last)
    spec = jnp.concatenate([spec, jnp.zeros((192, 32), F32)], axis=1)

    turned = [spec] + [pltpu.roll(spec, 32 * k, 1) for k in (1, 2, 3)]
    quarter = iota((16, 128), 1) // 32
    for g in range(3):
        for t in range(3):
            tile = None
            for n in range(4):
                at = 16 * (4 * g + n)
                piece = turned[(n - t) % 4][at : at + 16]
                tile = piece if tile is None else jnp.where(quarter == n, piece, tile)
            c_send[3 * g + t] = tile

    pl.semaphore_wait(barrier, NCOL - 1 + NROW - 1)

    def c_copy(w, dst):
        return pltpu.make_async_remote_copy(
            c_send.at[w], c_recv.at[c], ssem.at[0], rsem.at[0], device_id={"col": dst}, device_id_type=MESH
        )

    def start_c(k, carry):
        w = lax.rem(zw + k, ZW)
        dst = (NCOL * w) // ZW

        @pl.when(dst != c)
        def _():
            c_copy(w, dst).start()

        return carry

    lax.fori_loop(0, ZW, start_c, 0)

    kappa = iota((1, 256), 1)
    order = key_orders(kappa // 4, (kappa // 2) % 2, first_col)
    parity = (kappa % 2).astype(F32)
    hi, lo = split(fourier(iota((NLON, 256), 0).astype(F32), order, parity))
    fz_hi[...] = hi
    fz_lo[...] = lo

    def synthesize(t_hi, t_lo, x):
        x_hi, x_lo = split(x)
        return mm(t_hi[...], x_hi) + mm(t_hi[...], x_lo) + mm(t_lo[...], x_hi)

    def d_copy(dst):
        return pltpu.make_async_remote_copy(
            d_send.at[dst], d_recv.at[zw], ssem.at[1], rsem.at[1], device_id={"col": dst}, device_id_type=MESH
        )

    @pl.when(z_works)
    def _():
        c_recv[c] = c_send[zw]
        pltpu.make_async_copy(c_recv.at[0 : NCOL - 1], c_recv.at[0 : NCOL - 1], rsem.at[0]).wait()
        got = synthesize(fz_hi, fz_lo, c_recv[...].reshape(256, 128))
        d_send[...] = got.reshape(NCOL, 24, 128)

        def start_d(k, carry):
            d_copy(lax.rem(c + k, NCOL)).start()
            return carry

        lax.fori_loop(1, NCOL, start_d, 0)
        d_recv[zw] = d_send[c]

    place = iota((512, 1), 0)
    lon = 12 * (place // 16) + place % 16
    hi, lo = split(fourier(lon.astype(F32), order, parity))
    fr_hi[...] = hi
    fr_lo[...] = lo

    @pl.when(z_works)
    def _():
        pltpu.make_async_copy(d_recv.at[0 : ZW - 1], d_recv.at[0 : ZW - 1], rsem.at[1]).wait()

    @pl.when(jnp.logical_not(z_works))
    def _():
        pltpu.make_async_copy(d_recv, d_recv, rsem.at[1]).wait()

    x = d_recv[...].reshape(24 * ZW, 128)
    sub, ln = iota((24 * ZW, 128), 0), iota((24 * ZW, 128), 1)
    for s in (1, 2, 4):
        sbit, lbit = (sub & s) != 0, (ln & s) != 0
        down = pltpu.roll(pltpu.roll(x, s, 0), 128 - s, 1)
        up = pltpu.roll(pltpu.roll(x, 24 * ZW - s, 0), s, 1)
        x = jnp.where(sbit == lbit, x, jnp.where(sbit, down, up))
    a_send[...] = x.reshape(RW, 8, 128)

    def a_copy(v, dst):
        return pltpu.make_async_remote_copy(
            a_send.at[v], a_recv.at[r], ssem.at[2], rsem.at[2], device_id={"row": dst}, device_id_type=MESH
        )

    def start_a(k, carry):
        v = lax.rem(rw + k, RW)
        dst = (NROW * v) // RW

        @pl.when(dst != r)
        def _():
            a_copy(v, dst).start()

        return carry

    lax.fori_loop(0, RW, start_a, 0)

    for g in range(3):
        u, v = iota((128, 512), 0), iota((128, 512), 1)
        goes = 128 * ((u // 8) % 4) + 12 * (u % 8) + 4 * g + u // 32
        perm[128 * g : 128 * g + 128] = jnp.where(goes == v, 1.0, 0.0).astype(BF16)

    def b_copy(dst):
        return pltpu.make_async_remote_copy(
            b_send.at[dst], b_recv.at[rw], ssem.at[3], rsem.at[3], device_id={"row": dst}, device_id_type=MESH
        )

    @pl.when(r_works)
    def _():
        a_recv[r] = a_send[rw]
        pltpu.make_async_copy(a_recv.at[0 : NROW - 1], a_recv.at[0 : NROW - 1], rsem.at[2]).wait()
        got = synthesize(fr_hi, fr_lo, a_recv[...].reshape(256, 128))
        b_send[...] = got.reshape(NROW, 16, 128)

        def start_b(k, carry):
            b_copy(lax.rem(r + k, NROW)).start()
            return carry

        lax.fori_loop(1, NROW, start_b, 0)
        b_recv[rw] = b_send[r]
        pltpu.make_async_copy(b_recv.at[0 : RW - 1], b_recv.at[0 : RW - 1], rsem.at[3]).wait()

    @pl.when(jnp.logical_not(r_works))
    def _():
        pltpu.make_async_copy(b_recv, b_recv, rsem.at[3]).wait()

    x_hi, x_lo = split(b_recv[...].reshape(3, 144, 128))
    grid = None
    for g in range(3):
        p_g = perm[128 * g : 128 * g + 128]
        part = mm(x_hi[g], p_g) + mm(x_lo[g], p_g)
        grid = part if grid is None else grid + part
    ln = iota((16, 128), 1)
    for t in range(3):
        for n in range(4):
            z0, z1, z2 = (
                grid[48 * t + 16 * k : 48 * t + 16 * k + 16, 128 * n : 128 * n + 128] for k in range(3)
            )
            z1, z2 = pltpu.roll(z1, 96, 1), pltpu.roll(z2, 64, 1)
            o0 = jnp.where(ln < 96, z0, z1)
            o1 = jnp.where(ln < 64, z1, z2)
            rows = pl.ds(4 * t + n, 12, stride=12)
            oa[rows, :] = o0[0:12]
            ob[rows, :] = o1[0:12]
            oc[rows, :] = z2[0:12]
    out[:, 0:128] = oa[...]
    out[:, 128:256] = ob[...]
    out[:, 256:288] = oc[...][:, 0:32]

    @pl.when(z_works)
    def _():
        pltpu.make_async_copy(c_send.at[0 : ZW - 1], c_send.at[0 : ZW - 1], ssem.at[0]).wait()
        pltpu.make_async_copy(d_send.at[0 : NCOL - 1], d_send.at[0 : NCOL - 1], ssem.at[1]).wait()

    @pl.when(jnp.logical_not(z_works))
    def _():
        pltpu.make_async_copy(c_send, c_send, ssem.at[0]).wait()

    @pl.when(r_works)
    def _():
        pltpu.make_async_copy(a_send.at[0 : RW - 1], a_send.at[0 : RW - 1], ssem.at[2]).wait()
        pltpu.make_async_copy(b_send.at[0 : NROW - 1], b_send.at[0 : NROW - 1], ssem.at[3]).wait()

    @pl.when(jnp.logical_not(r_works))
    def _():
        pltpu.make_async_copy(a_send, a_send, ssem.at[2]).wait()


def on_device(covariance, coef_index):
    v = pltpu.VMEM
    return pl.pallas_call(
        kernel,
        out_shape=jax.ShapeDtypeStruct((144, 288), F32),
        in_specs=[pl.BlockSpec(memory_space=pl.ANY)] * 2,
        out_specs=pl.BlockSpec(memory_space=pltpu.VMEM),
        scratch_shapes=[
            v((512, 1024), BF16),
            v((3, 16384), I32),
            v((64, 128), F32),
            v((LL, LANES), F32),
            v((LL, LANES), F32),
            v((LL, LANES), F32),
            v((LL, LANES), F32),
            v((NLON, 256), BF16),
            v((NLON, 256), BF16),
            v((512, 256), BF16),
            v((512, 256), BF16),
            v((384, 512), BF16),
            v((ZW, 16, 128), F32),
            v((NCOL, 16, 128), F32),
            v((NCOL, 24, 128), F32),
            v((ZW, 24, 128), F32),
            v((RW, 8, 128), F32),
            v((NROW, 8, 128), F32),
            v((NROW, 16, 128), F32),
            v((RW, 16, 128), F32),
            v((144, 128), F32),
            v((144, 128), F32),
            v((144, 128), F32),
            pltpu.SemaphoreType.DMA((2,)),
            pltpu.SemaphoreType.DMA((4,)),
            pltpu.SemaphoreType.DMA((4,)),
        ],
        compiler_params=pltpu.CompilerParams(collective_id=0, has_side_effects=True),
    )(covariance, coef_index)


def solution(mesh):
    return jax.shard_map(
        on_device,
        mesh=mesh,
        in_specs=(P("row", "col"), P()),
        out_specs=P("row", "col"),
        check_vma=False,
    )
```

```python
import math

import jax
import jax.numpy as jnp
from jax import lax
from jax.experimental import pallas as pl
from jax.experimental.pallas import tpu as pltpu
from jax.sharding import PartitionSpec as P

LL = 128
NLON = 384
NLAT = 12
F32 = jnp.float32
BF16 = jnp.bfloat16
I32 = jnp.int32
MESH = pl.DeviceIdType.MESH

NROW = 32
NCOL = 16
ZW = 9
RW = 27
ZONE = 13
LANES = 384


def iota(shape, dim):
    return lax.broadcasted_iota(I32, shape, dim)


def split(x):
    hi = x.astype(BF16)
    return hi, (x - hi.astype(F32)).astype(BF16)


def mm(a, b, dims=((1,), (0,))):
    return lax.dot_general(a, b, (dims, ((), ())), preferred_element_type=F32)


def key_orders(pair, second, firsts):
    n = pair.shape[1]
    hit = iota((64, n), 0) == pair
    first = jnp.sum(jnp.where(hit, firsts, 0.0), axis=0, keepdims=True)
    other = jnp.where(first == 0.0, 64.0, 128.0 - first)
    return jnp.where(second == 0, first, other)


def fourier(j, m, parity):
    x = j * m + (NLON - (NLON // 4) * parity)
    p = x - NLON * jnp.floor(x * (1.0 / NLON))
    s = jnp.abs(p - NLON / 2) - NLON / 4
    t = s * (2.0 * math.pi / NLON)
    t2 = t * t
    r = -1.0 / 39916800.0
    for c in (1.0 / 362880.0, -1.0 / 5040.0, 1.0 / 120.0, -1.0 / 6.0, 1.0):
        r = r * t2 + c
    return r * t


def col_worker(z):
    w = jnp.where(z >= ZONE, z - ZONE, z + (NCOL - ZONE))
    return w, w < ZW


def row_worker(y):
    return y, y < RW


def ring(a, b):
    return min((a - b) % 4, (b - a) % 4)


COL_STEPS = sorted(range(1, NCOL), key=lambda k: -min(k, NCOL - k))
D_ORDER = (4, 3, 2, 1, 0, 5, 6, 7, 15, 14, 8, 13, 9, 12, 10, 11)
ROW_STEPS = sorted(
    [(dy, dx, dc) for dy in range(4) for dx in range(4) for dc in range(2) if dy or dx or dc],
    key=lambda k: -(3 * ring(k[0], 0) + 3 * ring(k[1], 0) + k[2]),
)


def wrap(x, n):
    return jnp.where(x >= n, x - n, x)


def kernel(
    cov_hbm,
    coef_hbm,
    out,
    cov,
    coef,
    firsts,
    ta,
    tb,
    ts,
    tp,
    fz_hi,
    fz_lo,
    fr_hi,
    fr_lo,
    perm,
    c_send,
    c_recv,
    d_send,
    d_recv,
    a_send,
    a_recv,
    b_send,
    b_recv,
    oa,
    ob,
    oc,
    local_sem,
    ssem,
    rsem,
):
    r = lax.axis_index("row")
    c = lax.axis_index("col")
    zw, z_works = col_worker(c)
    rw, r_works = row_worker(r)
    core = lax.rem(r, 2)
    at_x, at_y = lax.rem(lax.div(r, 2), 4), lax.div(r, 8)
    ys, xs = [8 * wrap(at_y + k, 4) for k in range(4)], [2 * wrap(at_x + k, 4) for k in range(4)]
    cores = [core, 1 - core]

    def row_step(step):
        dy, dx, dc = step
        return ys[dy] + xs[dx] + cores[dc]


    coef_copy = pltpu.make_async_copy(coef_hbm, coef, local_sem.at[0])
    coef_copy.start()
    cov_copy = pltpu.make_async_copy(cov_hbm, cov, local_sem.at[1])
    cov_copy.start()

    b_recv[...] = jnp.zeros((RW, 16, 128), F32)
    barrier = pltpu.get_barrier_semaphore()

    def greet_col(k, carry):
        dst = wrap(c + k, NCOL)

        @pl.when(jnp.logical_or(z_works, col_worker(dst)[1]))
        def _():
            pl.semaphore_signal(barrier, inc=1, device_id={"col": dst}, device_id_type=MESH)

        return carry

    for step in ROW_STEPS:
        to_row = row_step(step)
        needs = jnp.logical_or(r_works, row_worker(to_row)[1])
        pl.when(needs)(
            lambda to_row=to_row: pl.semaphore_signal(
                barrier, inc=1, device_id={"row": to_row}, device_id_type=MESH
            )
        )
    lax.fori_loop(1, NCOL, greet_col, 0)

    coef_copy.wait()
    for p in range(64):
        firsts[p : p + 1, :] = coef[1:2, 256 * p : 256 * p + 128].astype(F32)
    first_col = firsts[...][:, 0:1]

    lane = iota((1, LANES), 1)
    on_row = lane < 128
    y = lane - 128
    lat = jnp.where(on_row, lane // 8, y // 16)
    key = jnp.where(on_row, lane % 8, y % 16)
    pair = jnp.where(on_row, 2 * r, 4 * c) + key // 4
    m = key_orders(pair, (key // 2) % 2, first_col)
    delta = (lat.astype(F32) - 5.5) * (math.pi / 192)
    d2 = delta * delta
    cos_t = -delta * (1.0 - d2 * (1.0 / 6.0) * (1.0 - d2 * (1.0 / 20.0) * (1.0 - d2 * (1.0 / 42.0))))
    sin_t = 1.0 - d2 * 0.5 * (1.0 - d2 * (1.0 / 12.0) * (1.0 - d2 * (1.0 / 30.0)))
    deg = iota((LL, LANES), 0).astype(F32)
    diff = deg - m
    total = deg + m
    above = diff > 0.0
    inv = 1.0 / jnp.maximum(diff * total, 1.0)
    a = jnp.sqrt(jnp.maximum((2.0 * deg - 1.0) * (2.0 * deg + 1.0), 0.0) * inv)
    b = jnp.sqrt(
        jnp.maximum((2.0 * deg + 1.0) * (total - 1.0) * (diff - 1.0), 0.0)
        * inv
        / jnp.maximum(2.0 * deg - 3.0, 1.0)
    )
    ta[...] = jnp.where(above, a * cos_t, 0.0)
    tb[...] = jnp.where(above, b, 0.0)
    growth = jnp.sqrt((2.0 * deg + 1.0) / jnp.maximum(2.0 * deg, 1.0))
    growth = jnp.where(deg == 1.0, math.sqrt(3.0), growth)
    ts[...] = jnp.where(deg == 0.0, 1.0, growth * sin_t)

    def advance(block, state):
        before, earlier, sect = state
        base = pl.multiple_of(block * 8, 8)
        av, bv, sv = (t[pl.ds(base, 8), :] for t in (ta, tb, ts))
        rows = []
        for s in range(8):
            sect = sect * sv[s : s + 1]
            here = (block * 8 + s).astype(F32)
            now = jnp.where(m == here, sect, av[s : s + 1] * before - bv[s : s + 1] * earlier)
            rows.append(now)
            before, earlier = now, before
        tp[pl.ds(base, 8), :] = jnp.concatenate(rows, axis=0)
        return before, earlier, sect

    zero = jnp.zeros((1, LANES), F32)
    lax.fori_loop(0, LL // 8, advance, (zero, zero, zero + 1.0))

    table = tp[...].T
    keys = (2.0 * jnp.broadcast_to(m, (LL, LANES)) + (key % 2).astype(F32)).T[:, 0:1]

    def places(row, n, at):
        return coef[row : row + 1, pl.ds(pl.multiple_of(at, 512), n)]

    row_at, col_at = 512 * r, 1024 * c
    pick = jnp.where(iota((LL, 512), 0) == places(0, 512, row_at), 1.0, 0.0).astype(BF16)
    row_keys = (2 * places(1, 512, row_at) + places(2, 512, row_at)).astype(F32)
    w_row = mm(table[0:96].astype(BF16), pick)
    w_row = jnp.where(keys[0:96] == row_keys, w_row, 0.0).astype(BF16)

    pick = jnp.where(iota((LL, 1024), 0) == places(0, 1024, col_at), 1.0, 0.0).astype(BF16)
    col_keys = (2 * places(1, 1024, col_at) + places(2, 1024, col_at)).astype(F32)
    hit = keys[128:320] == col_keys
    t_hi, t_lo = split(table[128:320])
    w_hi = jnp.where(hit, mm(t_hi, pick), 0.0).astype(BF16)
    w_lo = jnp.where(hit, mm(t_lo, pick), 0.0).astype(BF16)

    cov_copy.wait()
    f_hi, f_lo = split(mm(w_row, cov[...]))
    last = ((1,), (1,))
    spec = mm(w_hi, f_hi, last) + mm(w_lo, f_hi, last) + mm(w_hi, f_lo, last)
    spec = jnp.concatenate([spec, jnp.zeros((192, 32), F32)], axis=1)

    turned = [spec] + [pltpu.roll(spec, 32 * k, 1) for k in (1, 2, 3)]
    quarter = iota((16, 128), 1) // 32
    for g in range(3):
        for t in range(3):
            tile = None
            for n in range(4):
                at = 16 * (4 * g + n)
                piece = turned[(n - t) % 4][at : at + 16]
                tile = piece if tile is None else jnp.where(quarter == n, piece, tile)
            c_send[3 * g + t] = tile

    pl.semaphore_wait(barrier, jnp.where(z_works, NCOL - 1, ZW) + jnp.where(r_works, NROW - 1, RW))

    def c_copy(w, dst):
        return pltpu.make_async_remote_copy(
            c_send.at[w], c_recv.at[c], ssem.at[0], rsem.at[0], device_id={"col": dst}, device_id_type=MESH
        )

    for step in COL_STEPS:
        to_col = wrap(c + step, NCOL)
        w, works = col_worker(to_col)
        pl.when(works)(lambda w=w, to_col=to_col: c_copy(w, to_col).start())

    kappa = iota((1, 256), 1)
    order = key_orders(kappa // 4, (kappa // 2) % 2, first_col)
    parity = (kappa % 2).astype(F32)
    hi, lo = split(fourier(iota((NLON, 256), 0).astype(F32), order, parity))
    fz_hi[...] = hi
    fz_lo[...] = lo

    def synthesize(t_hi, t_lo, x):
        x_hi, x_lo = split(x)
        return mm(t_hi[...], x_hi) + mm(t_hi[...], x_lo) + mm(t_lo[...], x_hi)

    def d_copy(dst):
        return pltpu.make_async_remote_copy(
            d_send.at[dst], d_recv.at[zw], ssem.at[1], rsem.at[1], device_id={"col": dst}, device_id_type=MESH
        )

    @pl.when(z_works)
    def _():
        c_recv[c] = c_send[zw]
        pltpu.make_async_copy(c_recv.at[0 : NCOL - 1], c_recv.at[0 : NCOL - 1], rsem.at[0]).wait()
        got = synthesize(fz_hi, fz_lo, c_recv[...].reshape(256, 128))
        d_send[...] = got.reshape(NCOL, 24, 128)

        for dst in D_ORDER:
            pl.when(c != dst)(lambda dst=dst: d_copy(dst).start())
        d_recv[zw] = d_send[c]

    place = iota((512, 1), 0)
    lon = 12 * (place // 16) + place % 16
    hi, lo = split(fourier(lon.astype(F32), order, parity))
    fr_hi[...] = hi
    fr_lo[...] = lo

    @pl.when(z_works)
    def _():
        pltpu.make_async_copy(d_recv.at[0 : ZW - 1], d_recv.at[0 : ZW - 1], rsem.at[1]).wait()

    @pl.when(jnp.logical_not(z_works))
    def _():
        pltpu.make_async_copy(d_recv, d_recv, rsem.at[1]).wait()

    x = d_recv[...].reshape(24 * ZW, 128)
    sub, ln = iota((24 * ZW, 128), 0), iota((24 * ZW, 128), 1)
    for s in (1, 2, 4):
        sbit, lbit = (sub & s) != 0, (ln & s) != 0
        down = pltpu.roll(pltpu.roll(x, s, 0), 128 - s, 1)
        up = pltpu.roll(pltpu.roll(x, 24 * ZW - s, 0), s, 1)
        x = jnp.where(sbit == lbit, x, jnp.where(sbit, down, up))
    a_send[...] = x.reshape(RW, 8, 128)

    def a_copy(v, dst):
        return pltpu.make_async_remote_copy(
            a_send.at[v], a_recv.at[r], ssem.at[2], rsem.at[2], device_id={"row": dst}, device_id_type=MESH
        )

    for step in ROW_STEPS:
        to_row = row_step(step)
        v, works = row_worker(to_row)
        pl.when(works)(lambda v=v, to_row=to_row: a_copy(v, to_row).start())

    for g in range(3):
        u, v = iota((128, 512), 0), iota((128, 512), 1)
        goes = 128 * ((u // 8) % 4) + 12 * (u % 8) + 4 * g + u // 32
        perm[128 * g : 128 * g + 128] = jnp.where(goes == v, 1.0, 0.0).astype(BF16)

    def b_copy(dst):
        return pltpu.make_async_remote_copy(
            b_send.at[dst, 0:12], b_recv.at[rw, 0:12], ssem.at[3], rsem.at[3], device_id={"row": dst}, device_id_type=MESH
        )

    @pl.when(r_works)
    def _():
        a_recv[r] = a_send[rw]
        pltpu.make_async_copy(a_recv.at[0 : NROW - 1], a_recv.at[0 : NROW - 1], rsem.at[2]).wait()
        got = synthesize(fr_hi, fr_lo, a_recv[...].reshape(256, 128))
        b_send[...] = got.reshape(NROW, 16, 128)

        for step in ROW_STEPS:
            b_copy(row_step(step)).start()
        b_recv[rw] = b_send[r]
        pltpu.make_async_copy(b_recv.at[0 : RW - 1, 0:12], b_recv.at[0 : RW - 1, 0:12], rsem.at[3]).wait()

    @pl.when(jnp.logical_not(r_works))
    def _():
        pltpu.make_async_copy(b_recv.at[:, 0:12], b_recv.at[:, 0:12], rsem.at[3]).wait()

    x_hi, x_lo = split(b_recv[...].reshape(3, 144, 128))
    grid = None
    for g in range(3):
        p_g = perm[128 * g : 128 * g + 128]
        part = mm(x_hi[g], p_g) + mm(x_lo[g], p_g)
        grid = part if grid is None else grid + part
    ln = iota((16, 128), 1)
    for t in range(3):
        for n in range(4):
            z0, z1, z2 = (
                grid[48 * t + 16 * k : 48 * t + 16 * k + 16, 128 * n : 128 * n + 128] for k in range(3)
            )
            z1, z2 = pltpu.roll(z1, 96, 1), pltpu.roll(z2, 64, 1)
            o0 = jnp.where(ln < 96, z0, z1)
            o1 = jnp.where(ln < 64, z1, z2)
            rows = pl.ds(4 * t + n, 12, stride=12)
            oa[rows, :] = o0[0:12]
            ob[rows, :] = o1[0:12]
            oc[rows, :] = z2[0:12]
    out[:, 0:128] = oa[...]
    out[:, 128:256] = ob[...]
    out[:, 256:288] = oc[...][:, 0:32]

    @pl.when(z_works)
    def _():
        pltpu.make_async_copy(c_send.at[0 : ZW - 1], c_send.at[0 : ZW - 1], ssem.at[0]).wait()
        pltpu.make_async_copy(d_send.at[0 : NCOL - 1], d_send.at[0 : NCOL - 1], ssem.at[1]).wait()

    @pl.when(jnp.logical_not(z_works))
    def _():
        pltpu.make_async_copy(c_send, c_send, ssem.at[0]).wait()

    @pl.when(r_works)
    def _():
        pltpu.make_async_copy(a_send.at[0 : RW - 1], a_send.at[0 : RW - 1], ssem.at[2]).wait()
        pltpu.make_async_copy(b_send.at[0 : NROW - 1, 0:12], b_send.at[0 : NROW - 1, 0:12], ssem.at[3]).wait()

    @pl.when(jnp.logical_not(r_works))
    def _():
        pltpu.make_async_copy(a_send, a_send, ssem.at[2]).wait()


def on_device(covariance, coef_index):
    v = pltpu.VMEM
    return pl.pallas_call(
        kernel,
        out_shape=pltpu.VMEM((144, 288), F32),
        in_specs=[pl.BlockSpec(memory_space=pl.ANY)] * 2,
        out_specs=pl.BlockSpec(memory_space=pltpu.VMEM),
        scratch_shapes=[
            v((512, 1024), BF16),
            v((3, 16384), I32),
            v((64, 128), F32),
            v((LL, LANES), F32),
            v((LL, LANES), F32),
            v((LL, LANES), F32),
            v((LL, LANES), F32),
            v((NLON, 256), BF16),
            v((NLON, 256), BF16),
            v((512, 256), BF16),
            v((512, 256), BF16),
            v((384, 512), BF16),
            v((ZW, 16, 128), F32),
            v((NCOL, 16, 128), F32),
            v((NCOL, 24, 128), F32),
            v((ZW, 24, 128), F32),
            v((RW, 8, 128), F32),
            v((NROW, 8, 128), F32),
            v((NROW, 16, 128), F32),
            v((RW, 16, 128), F32),
            v((144, 128), F32),
            v((144, 128), F32),
            v((144, 128), F32),
            pltpu.SemaphoreType.DMA((2,)),
            pltpu.SemaphoreType.DMA((4,)),
            pltpu.SemaphoreType.DMA((4,)),
        ],
        compiler_params=pltpu.CompilerParams(collective_id=0, has_side_effects=True),
    )(covariance, coef_index)


def solution(mesh):
    return jax.shard_map(
        on_device,
        mesh=mesh,
        in_specs=(P("row", "col"), P()),
        out_specs=P("row", "col"),
        check_vma=False,
    )
```

```python
import math

import jax
import jax.numpy as jnp
from jax import lax
from jax.experimental import pallas as pl
from jax.experimental.pallas import tpu as pltpu
from jax.sharding import PartitionSpec as P

LL = 128
NLON = 384
NLAT = 12
F32 = jnp.float32
BF16 = jnp.bfloat16
I32 = jnp.int32
MESH = pl.DeviceIdType.MESH

NROW = 32
NCOL = 16
ZW = 9
RW = 27
WORKERS = (0, 1, 15, 3, 13, 4, 12, 6, 7)
LANES = 384


def iota(shape, dim):
    return lax.broadcasted_iota(I32, shape, dim)


def split(x):
    hi = x.astype(BF16)
    return hi, (x - hi.astype(F32)).astype(BF16)


def mm(a, b, dims=((1,), (0,))):
    return lax.dot_general(a, b, (dims, ((), ())), preferred_element_type=F32)


def key_orders(pair, second, firsts):
    n = pair.shape[1]
    hit = iota((64, n), 0) == pair
    first = jnp.sum(jnp.where(hit, firsts, 0.0), axis=0, keepdims=True)
    other = jnp.where(first == 0.0, 64.0, 128.0 - first)
    return jnp.where(second == 0, first, other)


def fourier(j, m, parity):
    x = j * m + (NLON - (NLON // 4) * parity)
    p = x - NLON * jnp.floor(x * (1.0 / NLON))
    s = jnp.abs(p - NLON / 2) - NLON / 4
    t = s * (2.0 * math.pi / NLON)
    t2 = t * t
    r = -1.0 / 39916800.0
    for c in (1.0 / 362880.0, -1.0 / 5040.0, 1.0 / 120.0, -1.0 / 6.0, 1.0):
        r = r * t2 + c
    return r * t


def col_worker(z):
    w, works = 0, False
    for k, at in enumerate(WORKERS):
        w, works = jnp.where(z == at, k, w), jnp.logical_or(works, z == at)
    return w, works


def row_worker(y):
    return y, y < RW


def ring(a, b):
    return min((a - b) % 4, (b - a) % 4)


COL_STEPS = sorted(range(1, NCOL), key=lambda k: -min(k, NCOL - k))
D_ORDER = (0, 1, 2, 3, 4, 5, 6, 7, 15, 14, 13, 8, 12, 9, 10, 11)
ROW_STEPS = sorted(
    [(dy, dx, dc) for dy in range(4) for dx in range(4) for dc in range(2) if dy or dx or dc],
    key=lambda k: -(3 * ring(k[0], 0) + 3 * ring(k[1], 0) + k[2]),
)


def wrap(x, n):
    return jnp.where(x >= n, x - n, x)


def kernel(
    cov_hbm,
    coef_hbm,
    out,
    cov,
    coef,
    firsts,
    ta,
    tb,
    ts,
    tp,
    fz_hi,
    fz_lo,
    fr_hi,
    fr_lo,
    perm,
    c_send,
    c_recv,
    d_send,
    d_recv,
    a_send,
    a_recv,
    b_send,
    b_recv,
    oa,
    ob,
    oc,
    local_sem,
    ssem,
    rsem,
):
    r = lax.axis_index("row")
    c = lax.axis_index("col")
    zw, z_works = col_worker(c)
    rw, r_works = row_worker(r)
    core = lax.rem(r, 2)
    at_x, at_y = lax.rem(lax.div(r, 2), 4), lax.div(r, 8)
    ys, xs = [8 * wrap(at_y + k, 4) for k in range(4)], [2 * wrap(at_x + k, 4) for k in range(4)]
    cores = [core, 1 - core]

    def row_step(step):
        dy, dx, dc = step
        return ys[dy] + xs[dx] + cores[dc]


    coef_copy = pltpu.make_async_copy(coef_hbm, coef, local_sem.at[0])
    coef_copy.start()
    cov_copy = pltpu.make_async_copy(cov_hbm, cov, local_sem.at[1])
    cov_copy.start()

    b_recv[...] = jnp.zeros((RW, 16, 128), F32)
    barrier = pltpu.get_barrier_semaphore()

    for step in ROW_STEPS:
        to_row = row_step(step)
        needs = jnp.logical_or(r_works, row_worker(to_row)[1])
        pl.when(needs)(
            lambda to_row=to_row: pl.semaphore_signal(
                barrier, inc=1, device_id={"row": to_row}, device_id_type=MESH
            )
        )
    for z in range(NCOL):
        needs = c != z if z in WORKERS else z_works
        pl.when(needs)(
            lambda z=z: pl.semaphore_signal(barrier, inc=1, device_id={"col": z}, device_id_type=MESH)
        )

    coef_copy.wait()
    for p in range(64):
        firsts[p : p + 1, :] = coef[1:2, 256 * p : 256 * p + 128].astype(F32)
    first_col = firsts[...][:, 0:1]

    lane = iota((1, LANES), 1)
    on_row = lane < 128
    y = lane - 128
    lat = jnp.where(on_row, lane // 8, y // 16)
    key = jnp.where(on_row, lane % 8, y % 16)
    pair = jnp.where(on_row, 2 * r, 4 * c) + key // 4
    m = key_orders(pair, (key // 2) % 2, first_col)
    delta = (lat.astype(F32) - 5.5) * (math.pi / 192)
    d2 = delta * delta
    cos_t = -delta * (1.0 - d2 * (1.0 / 6.0) * (1.0 - d2 * (1.0 / 20.0) * (1.0 - d2 * (1.0 / 42.0))))
    sin_t = 1.0 - d2 * 0.5 * (1.0 - d2 * (1.0 / 12.0) * (1.0 - d2 * (1.0 / 30.0)))
    deg = iota((LL, LANES), 0).astype(F32)
    diff = deg - m
    total = deg + m
    above = diff > 0.0
    inv = 1.0 / jnp.maximum(diff * total, 1.0)
    a = jnp.sqrt(jnp.maximum((2.0 * deg - 1.0) * (2.0 * deg + 1.0), 0.0) * inv)
    b = jnp.sqrt(
        jnp.maximum((2.0 * deg + 1.0) * (total - 1.0) * (diff - 1.0), 0.0)
        * inv
        / jnp.maximum(2.0 * deg - 3.0, 1.0)
    )
    ta[...] = jnp.where(above, a * cos_t, 0.0)
    tb[...] = jnp.where(above, b, 0.0)
    growth = jnp.sqrt((2.0 * deg + 1.0) / jnp.maximum(2.0 * deg, 1.0))
    growth = jnp.where(deg == 1.0, math.sqrt(3.0), growth)
    ts[...] = jnp.where(deg == 0.0, 1.0, growth * sin_t)

    def advance(block, state):
        before, earlier, sect = state
        base = pl.multiple_of(block * 8, 8)
        av, bv, sv = (t[pl.ds(base, 8), :] for t in (ta, tb, ts))
        rows = []
        for s in range(8):
            sect = sect * sv[s : s + 1]
            here = (block * 8 + s).astype(F32)
            now = jnp.where(m == here, sect, av[s : s + 1] * before - bv[s : s + 1] * earlier)
            rows.append(now)
            before, earlier = now, before
        tp[pl.ds(base, 8), :] = jnp.concatenate(rows, axis=0)
        return before, earlier, sect

    zero = jnp.zeros((1, LANES), F32)
    lax.fori_loop(0, LL // 8, advance, (zero, zero, zero + 1.0))

    table = tp[...].T
    keys = (2.0 * jnp.broadcast_to(m, (LL, LANES)) + (key % 2).astype(F32)).T[:, 0:1]

    def places(row, n, at):
        return coef[row : row + 1, pl.ds(pl.multiple_of(at, 512), n)]

    row_at, col_at = 512 * r, 1024 * c
    pick = jnp.where(iota((LL, 512), 0) == places(0, 512, row_at), 1.0, 0.0).astype(BF16)
    row_keys = (2 * places(1, 512, row_at) + places(2, 512, row_at)).astype(F32)
    w_row = mm(table[0:96].astype(BF16), pick)
    w_row = jnp.where(keys[0:96] == row_keys, w_row, 0.0).astype(BF16)

    pick = jnp.where(iota((LL, 1024), 0) == places(0, 1024, col_at), 1.0, 0.0).astype(BF16)
    col_keys = (2 * places(1, 1024, col_at) + places(2, 1024, col_at)).astype(F32)
    hit = keys[128:320] == col_keys
    t_hi, t_lo = split(table[128:320])
    w_hi = jnp.where(hit, mm(t_hi, pick), 0.0).astype(BF16)
    w_lo = jnp.where(hit, mm(t_lo, pick), 0.0).astype(BF16)

    cov_copy.wait()
    f_hi, f_lo = split(mm(w_row, cov[...]))
    last = ((1,), (1,))
    spec = mm(w_hi, f_hi, last) + mm(w_lo, f_hi, last) + mm(w_hi, f_lo, last)
    spec = jnp.concatenate([spec, jnp.zeros((192, 32), F32)], axis=1)

    turned = [spec] + [pltpu.roll(spec, 32 * k, 1) for k in (1, 2, 3)]
    quarter = iota((16, 128), 1) // 32
    for g in range(3):
        for t in range(3):
            tile = None
            for n in range(4):
                at = 16 * (4 * g + n)
                piece = turned[(n - t) % 4][at : at + 16]
                tile = piece if tile is None else jnp.where(quarter == n, piece, tile)
            c_send[3 * g + t] = tile

    pl.semaphore_wait(barrier, jnp.where(z_works, NCOL - 1, ZW) + jnp.where(r_works, NROW - 1, RW))

    def c_copy(w, dst):
        return pltpu.make_async_remote_copy(
            c_send.at[w], c_recv.at[c], ssem.at[0], rsem.at[0], device_id={"col": dst}, device_id_type=MESH
        )

    for step in COL_STEPS:
        to_col = wrap(c + step, NCOL)
        w, works = col_worker(to_col)
        pl.when(works)(lambda w=w, to_col=to_col: c_copy(w, to_col).start())

    kappa = iota((1, 256), 1)
    order = key_orders(kappa // 4, (kappa // 2) % 2, first_col)
    parity = (kappa % 2).astype(F32)
    hi, lo = split(fourier(iota((NLON, 256), 0).astype(F32), order, parity))
    fz_hi[...] = hi
    fz_lo[...] = lo

    def synthesize(t_hi, t_lo, x):
        x_hi, x_lo = split(x)
        return mm(t_hi[...], x_hi) + mm(t_hi[...], x_lo) + mm(t_lo[...], x_hi)

    def d_copy(dst):
        return pltpu.make_async_remote_copy(
            d_send.at[dst], d_recv.at[zw], ssem.at[1], rsem.at[1], device_id={"col": dst}, device_id_type=MESH
        )

    @pl.when(z_works)
    def _():
        c_recv[c] = c_send[zw]
        pltpu.make_async_copy(c_recv.at[0 : NCOL - 1], c_recv.at[0 : NCOL - 1], rsem.at[0]).wait()
        got = synthesize(fz_hi, fz_lo, c_recv[...].reshape(256, 128))
        d_send[...] = got.reshape(NCOL, 24, 128)

        for dst in D_ORDER:
            pl.when(c != dst)(lambda dst=dst: d_copy(dst).start())
        d_recv[zw] = d_send[c]

    place = iota((512, 1), 0)
    lon = 12 * (place // 16) + place % 16
    hi, lo = split(fourier(lon.astype(F32), order, parity))
    fr_hi[...] = hi
    fr_lo[...] = lo

    @pl.when(z_works)
    def _():
        pltpu.make_async_copy(d_recv.at[0 : ZW - 1], d_recv.at[0 : ZW - 1], rsem.at[1]).wait()

    @pl.when(jnp.logical_not(z_works))
    def _():
        pltpu.make_async_copy(d_recv, d_recv, rsem.at[1]).wait()

    x = d_recv[...].reshape(24 * ZW, 128)
    sub, ln = iota((24 * ZW, 128), 0), iota((24 * ZW, 128), 1)
    for s in (1, 2, 4):
        sbit, lbit = (sub & s) != 0, (ln & s) != 0
        down = pltpu.roll(pltpu.roll(x, s, 0), 128 - s, 1)
        up = pltpu.roll(pltpu.roll(x, 24 * ZW - s, 0), s, 1)
        x = jnp.where(sbit == lbit, x, jnp.where(sbit, down, up))
    a_send[...] = x.reshape(RW, 8, 128)

    def a_copy(v, dst):
        return pltpu.make_async_remote_copy(
            a_send.at[v], a_recv.at[r], ssem.at[2], rsem.at[2], device_id={"row": dst}, device_id_type=MESH
        )

    for step in ROW_STEPS:
        to_row = row_step(step)
        v, works = row_worker(to_row)
        pl.when(works)(lambda v=v, to_row=to_row: a_copy(v, to_row).start())

    for g in range(3):
        u, v = iota((128, 512), 0), iota((128, 512), 1)
        goes = 128 * ((u // 8) % 4) + 12 * (u % 8) + 4 * g + u // 32
        perm[128 * g : 128 * g + 128] = jnp.where(goes == v, 1.0, 0.0).astype(BF16)

    def b_copy(dst):
        return pltpu.make_async_remote_copy(
            b_send.at[dst, 0:12], b_recv.at[rw, 0:12], ssem.at[3], rsem.at[3], device_id={"row": dst}, device_id_type=MESH
        )

    @pl.when(r_works)
    def _():
        a_recv[r] = a_send[rw]
        pltpu.make_async_copy(a_recv.at[0 : NROW - 1], a_recv.at[0 : NROW - 1], rsem.at[2]).wait()
        got = synthesize(fr_hi, fr_lo, a_recv[...].reshape(256, 128))
        b_send[...] = got.reshape(NROW, 16, 128)

        for step in ROW_STEPS:
            b_copy(row_step(step)).start()
        b_recv[rw] = b_send[r]
        pltpu.make_async_copy(b_recv.at[0 : RW - 1, 0:12], b_recv.at[0 : RW - 1, 0:12], rsem.at[3]).wait()

    @pl.when(jnp.logical_not(r_works))
    def _():
        pltpu.make_async_copy(b_recv.at[:, 0:12], b_recv.at[:, 0:12], rsem.at[3]).wait()

    x_hi, x_lo = split(b_recv[...].reshape(3, 144, 128))
    grid = None
    for g in range(3):
        p_g = perm[128 * g : 128 * g + 128]
        part = mm(x_hi[g], p_g) + mm(x_lo[g], p_g)
        grid = part if grid is None else grid + part
    ln = iota((16, 128), 1)
    for t in range(3):
        for n in range(4):
            z0, z1, z2 = (
                grid[48 * t + 16 * k : 48 * t + 16 * k + 16, 128 * n : 128 * n + 128] for k in range(3)
            )
            z1, z2 = pltpu.roll(z1, 96, 1), pltpu.roll(z2, 64, 1)
            o0 = jnp.where(ln < 96, z0, z1)
            o1 = jnp.where(ln < 64, z1, z2)
            rows = pl.ds(4 * t + n, 12, stride=12)
            oa[rows, :] = o0[0:12]
            ob[rows, :] = o1[0:12]
            oc[rows, :] = z2[0:12]
    out[:, 0:128] = oa[...]
    out[:, 128:256] = ob[...]
    out[:, 256:288] = oc[...][:, 0:32]

    @pl.when(z_works)
    def _():
        pltpu.make_async_copy(c_send.at[0 : ZW - 1], c_send.at[0 : ZW - 1], ssem.at[0]).wait()
        pltpu.make_async_copy(d_send.at[0 : NCOL - 1], d_send.at[0 : NCOL - 1], ssem.at[1]).wait()

    @pl.when(jnp.logical_not(z_works))
    def _():
        pltpu.make_async_copy(c_send, c_send, ssem.at[0]).wait()

    @pl.when(r_works)
    def _():
        pltpu.make_async_copy(a_send.at[0 : RW - 1], a_send.at[0 : RW - 1], ssem.at[2]).wait()
        pltpu.make_async_copy(b_send.at[0 : NROW - 1, 0:12], b_send.at[0 : NROW - 1, 0:12], ssem.at[3]).wait()

    @pl.when(jnp.logical_not(r_works))
    def _():
        pltpu.make_async_copy(a_send, a_send, ssem.at[2]).wait()


def on_device(covariance, coef_index):
    v = pltpu.VMEM
    return pl.pallas_call(
        kernel,
        out_shape=pltpu.VMEM((144, 288), F32),
        in_specs=[pl.BlockSpec(memory_space=pl.ANY)] * 2,
        out_specs=pl.BlockSpec(memory_space=pltpu.VMEM),
        scratch_shapes=[
            v((512, 1024), BF16),
            v((3, 16384), I32),
            v((64, 128), F32),
            v((LL, LANES), F32),
            v((LL, LANES), F32),
            v((LL, LANES), F32),
            v((LL, LANES), F32),
            v((NLON, 256), BF16),
            v((NLON, 256), BF16),
            v((512, 256), BF16),
            v((512, 256), BF16),
            v((384, 512), BF16),
            v((ZW, 16, 128), F32),
            v((NCOL, 16, 128), F32),
            v((NCOL, 24, 128), F32),
            v((ZW, 24, 128), F32),
            v((RW, 8, 128), F32),
            v((NROW, 8, 128), F32),
            v((NROW, 16, 128), F32),
            v((RW, 16, 128), F32),
            v((144, 128), F32),
            v((144, 128), F32),
            v((144, 128), F32),
            pltpu.SemaphoreType.DMA((2,)),
            pltpu.SemaphoreType.DMA((4,)),
            pltpu.SemaphoreType.DMA((4,)),
        ],
        compiler_params=pltpu.CompilerParams(collective_id=0, has_side_effects=True),
    )(covariance, coef_index)


def solution(mesh):
    return jax.shard_map(
        on_device,
        mesh=mesh,
        in_specs=(P("row", "col"), P()),
        out_specs=P("row", "col"),
        check_vma=False,
    )
```

```python
import math

import jax
import jax.numpy as jnp
from jax import lax
from jax.experimental import pallas as pl
from jax.experimental.pallas import tpu as pltpu
from jax.sharding import PartitionSpec as P

LL = 128
NLON = 384
NLAT = 12
F32 = jnp.float32
BF16 = jnp.bfloat16
I32 = jnp.int32
MESH = pl.DeviceIdType.MESH

NROW = 32
NCOL = 16
ZW = 9
RW = 27
WORKERS = (0, 1, 15, 3, 13, 4, 12, 6, 7)
LANES = 384


def iota(shape, dim):
    return lax.broadcasted_iota(I32, shape, dim)


def split(x):
    hi = x.astype(BF16)
    return hi, (x - hi.astype(F32)).astype(BF16)


def mm(a, b, dims=((1,), (0,))):
    return lax.dot_general(a, b, (dims, ((), ())), preferred_element_type=F32)


def key_orders(pair, second, firsts):
    n = pair.shape[1]
    hit = iota((64, n), 0) == pair
    first = jnp.sum(jnp.where(hit, firsts, 0.0), axis=0, keepdims=True)
    other = jnp.where(first == 0.0, 64.0, 128.0 - first)
    return jnp.where(second == 0, first, other)


def fourier(j, m, parity):
    x = j * m + (NLON - (NLON // 4) * parity)
    p = x - NLON * jnp.floor(x * (1.0 / NLON))
    s = jnp.abs(p - NLON / 2) - NLON / 4
    t = s * (2.0 * math.pi / NLON)
    t2 = t * t
    r = -1.0 / 39916800.0
    for c in (1.0 / 362880.0, -1.0 / 5040.0, 1.0 / 120.0, -1.0 / 6.0, 1.0):
        r = r * t2 + c
    return r * t


def col_worker(z):
    w, works = 0, False
    for k, at in enumerate(WORKERS):
        w, works = jnp.where(z == at, k, w), jnp.logical_or(works, z == at)
    return w, works


def row_worker(y):
    return y, y < RW


def ring(a, b):
    return min((a - b) % 4, (b - a) % 4)


COL_STEPS = sorted(range(1, NCOL), key=lambda k: -min(k, NCOL - k))
D_ORDER = (0, 1, 2, 3, 4, 5, 6, 7, 15, 14, 13, 8, 12, 9, 10, 11)
ROW_STEPS = sorted(
    [(dy, dx, dc) for dy in range(4) for dx in range(4) for dc in range(2) if dy or dx or dc],
    key=lambda k: -(3 * ring(k[0], 0) + 3 * ring(k[1], 0) + k[2]),
)


def wrap(x, n):
    return jnp.where(x >= n, x - n, x)


def kernel(
    cov_hbm,
    coef_hbm,
    out,
    cov,
    coef,
    firsts,
    ta,
    tb,
    ts,
    tp,
    fz_hi,
    fz_lo,
    fr_hi,
    fr_lo,
    perm,
    c_send,
    c_recv,
    d_send,
    d_recv,
    a_send,
    a_recv,
    b_send,
    b_recv,
    oa,
    ob,
    oc,
    local_sem,
    ssem,
    rsem,
):
    r = lax.axis_index("row")
    c = lax.axis_index("col")
    zw, z_works = col_worker(c)
    rw, r_works = row_worker(r)
    core = lax.rem(r, 2)
    at_x, at_y = lax.rem(lax.div(r, 2), 4), lax.div(r, 8)
    ys, xs = [8 * wrap(at_y + k, 4) for k in range(4)], [2 * wrap(at_x + k, 4) for k in range(4)]
    cores = [core, 1 - core]

    def row_step(step):
        dy, dx, dc = step
        return ys[dy] + xs[dx] + cores[dc]


    coef_copy = pltpu.make_async_copy(coef_hbm, coef, local_sem.at[0])
    coef_copy.start()
    cov_copy = pltpu.make_async_copy(cov_hbm, cov, local_sem.at[1])
    cov_copy.start()

    b_recv[...] = jnp.zeros((RW, 16, 128), F32)
    barrier = pltpu.get_barrier_semaphore()

    for step in ROW_STEPS:
        to_row = row_step(step)
        needs = jnp.logical_or(r_works, row_worker(to_row)[1])
        pl.when(needs)(
            lambda to_row=to_row: pl.semaphore_signal(
                barrier, inc=1, device_id={"row": to_row}, device_id_type=MESH
            )
        )
    for z in range(NCOL):
        needs = c != z if z in WORKERS else z_works
        pl.when(needs)(
            lambda z=z: pl.semaphore_signal(barrier, inc=1, device_id={"col": z}, device_id_type=MESH)
        )

    coef_copy.wait()
    for p in range(64):
        firsts[p : p + 1, :] = coef[1:2, 256 * p : 256 * p + 128].astype(F32)
    first_col = firsts[...][:, 0:1]

    lane = iota((1, LANES), 1)
    on_row = lane < 128
    y = lane - 128
    lat = jnp.where(on_row, lane // 8, y // 16)
    key = jnp.where(on_row, lane % 8, y % 16)
    pair = jnp.where(on_row, 2 * r, 4 * c) + key // 4
    m = key_orders(pair, (key // 2) % 2, first_col)
    delta = (lat.astype(F32) - 5.5) * (math.pi / 192)
    d2 = delta * delta
    cos_t = -delta * (1.0 - d2 * (1.0 / 6.0) * (1.0 - d2 * (1.0 / 20.0) * (1.0 - d2 * (1.0 / 42.0))))
    sin_t = 1.0 - d2 * 0.5 * (1.0 - d2 * (1.0 / 12.0) * (1.0 - d2 * (1.0 / 30.0)))
    deg = iota((LL, LANES), 0).astype(F32)
    diff = deg - m
    total = deg + m
    above = diff > 0.0
    inv = 1.0 / jnp.maximum(diff * total, 1.0)
    a = jnp.sqrt(jnp.maximum((2.0 * deg - 1.0) * (2.0 * deg + 1.0), 0.0) * inv)
    b = jnp.sqrt(
        jnp.maximum((2.0 * deg + 1.0) * (total - 1.0) * (diff - 1.0), 0.0)
        * inv
        / jnp.maximum(2.0 * deg - 3.0, 1.0)
    )
    ta[...] = jnp.where(above, a * cos_t, 0.0)
    tb[...] = jnp.where(above, b, 0.0)
    growth = jnp.sqrt((2.0 * deg + 1.0) / jnp.maximum(2.0 * deg, 1.0))
    growth = jnp.where(deg == 1.0, math.sqrt(3.0), growth)
    ts[...] = jnp.where(deg == 0.0, 1.0, growth * sin_t)

    def advance(block, state):
        before, earlier, sect = state
        base = pl.multiple_of(block * 8, 8)
        av, bv, sv = (t[pl.ds(base, 8), :] for t in (ta, tb, ts))
        rows = []
        for s in range(8):
            sect = sect * sv[s : s + 1]
            here = (block * 8 + s).astype(F32)
            now = jnp.where(m == here, sect, av[s : s + 1] * before - bv[s : s + 1] * earlier)
            rows.append(now)
            before, earlier = now, before
        tp[pl.ds(base, 8), :] = jnp.concatenate(rows, axis=0)
        return before, earlier, sect

    zero = jnp.zeros((1, LANES), F32)
    lax.fori_loop(0, LL // 8, advance, (zero, zero, zero + 1.0))

    table = tp[...].T
    keys = (2.0 * jnp.broadcast_to(m, (LL, LANES)) + (key % 2).astype(F32)).T[:, 0:1]

    def places(row, n, at):
        return coef[row : row + 1, pl.ds(pl.multiple_of(at, 512), n)]

    row_at, col_at = 512 * r, 1024 * c
    pick = jnp.where(iota((LL, 512), 0) == places(0, 512, row_at), 1.0, 0.0).astype(BF16)
    row_keys = (2 * places(1, 512, row_at) + places(2, 512, row_at)).astype(F32)
    w_row = mm(table[0:96].astype(BF16), pick)
    w_row = jnp.where(keys[0:96] == row_keys, w_row, 0.0).astype(BF16)

    pick = jnp.where(iota((LL, 1024), 0) == places(0, 1024, col_at), 1.0, 0.0).astype(BF16)
    col_keys = (2 * places(1, 1024, col_at) + places(2, 1024, col_at)).astype(F32)
    hit = keys[128:320] == col_keys
    t_hi, t_lo = split(table[128:320])
    w_hi = jnp.where(hit, mm(t_hi, pick), 0.0).astype(BF16)
    w_lo = jnp.where(hit, mm(t_lo, pick), 0.0).astype(BF16)

    cov_copy.wait()
    f_hi, f_lo = split(mm(w_row, cov[...]))
    last = ((1,), (1,))
    spec = mm(w_hi, f_hi, last) + mm(w_lo, f_hi, last) + mm(w_hi, f_lo, last)
    spec = jnp.concatenate([spec, jnp.zeros((192, 32), F32)], axis=1)

    turned = [spec] + [pltpu.roll(spec, 32 * k, 1) for k in (1, 2, 3)]
    quarter = iota((16, 128), 1) // 32
    for g in range(3):
        for t in range(3):
            tile = None
            for n in range(4):
                at = 16 * (4 * g + n)
                piece = turned[(n - t) % 4][at : at + 16]
                tile = piece if tile is None else jnp.where(quarter == n, piece, tile)
            c_send[3 * g + t] = tile

    pl.semaphore_wait(barrier, jnp.where(z_works, NCOL - 1, ZW) + jnp.where(r_works, NROW - 1, RW))

    def c_copy(w, dst):
        return pltpu.make_async_remote_copy(
            c_send.at[w], c_recv.at[c], ssem.at[0], rsem.at[0], device_id={"col": dst}, device_id_type=MESH
        )

    for step in COL_STEPS:
        to_col = wrap(c + step, NCOL)
        w, works = col_worker(to_col)
        pl.when(works)(lambda w=w, to_col=to_col: c_copy(w, to_col).start())

    kappa = iota((1, 256), 1)
    order = key_orders(kappa // 4, (kappa // 2) % 2, first_col)
    parity = (kappa % 2).astype(F32)
    hi, lo = split(fourier(iota((NLON, 256), 0).astype(F32), order, parity))
    fz_hi[...] = hi
    fz_lo[...] = lo

    def synthesize(t_hi, t_lo, x):
        x_hi, x_lo = split(x)
        return mm(t_hi[...], x_hi) + mm(t_hi[...], x_lo) + mm(t_lo[...], x_hi)

    def d_copy(dst):
        return pltpu.make_async_remote_copy(
            d_send.at[dst], d_recv.at[zw], ssem.at[1], rsem.at[1], device_id={"col": dst}, device_id_type=MESH
        )

    @pl.when(z_works)
    def _():
        c_recv[c] = c_send[zw]
        pltpu.make_async_copy(c_recv.at[0 : NCOL - 1], c_recv.at[0 : NCOL - 1], rsem.at[0]).wait()
        got = synthesize(fz_hi, fz_lo, c_recv[...].reshape(256, 128))
        d_send[...] = got.reshape(NCOL, 24, 128)

        for dst in D_ORDER[:8]:
            pl.when(c != dst)(lambda dst=dst: d_copy(dst).start())
        d_recv[zw] = d_send[c]

    place = iota((512, 1), 0)
    lon = 12 * (place // 16) + place % 16
    hi, lo = split(fourier(lon.astype(F32), order, parity))
    fr_hi[...] = hi
    fr_lo[...] = lo

    @pl.when(z_works)
    def _():
        for dst in D_ORDER[8:]:
            pl.when(c != dst)(lambda dst=dst: d_copy(dst).start())

    @pl.when(z_works)
    def _():
        pltpu.make_async_copy(d_recv.at[0 : ZW - 1], d_recv.at[0 : ZW - 1], rsem.at[1]).wait()

    @pl.when(jnp.logical_not(z_works))
    def _():
        pltpu.make_async_copy(d_recv, d_recv, rsem.at[1]).wait()

    x = d_recv[...].reshape(24 * ZW, 128)
    sub, ln = iota((24 * ZW, 128), 0), iota((24 * ZW, 128), 1)
    for s in (1, 2, 4):
        sbit, lbit = (sub & s) != 0, (ln & s) != 0
        down = pltpu.roll(pltpu.roll(x, s, 0), 128 - s, 1)
        up = pltpu.roll(pltpu.roll(x, 24 * ZW - s, 0), s, 1)
        x = jnp.where(sbit == lbit, x, jnp.where(sbit, down, up))
    a_send[...] = x.reshape(RW, 8, 128)

    def a_copy(v, dst):
        return pltpu.make_async_remote_copy(
            a_send.at[v], a_recv.at[r], ssem.at[2], rsem.at[2], device_id={"row": dst}, device_id_type=MESH
        )

    for step in ROW_STEPS:
        to_row = row_step(step)
        v, works = row_worker(to_row)
        pl.when(works)(lambda v=v, to_row=to_row: a_copy(v, to_row).start())

    for g in range(3):
        u, v = iota((128, 512), 0), iota((128, 512), 1)
        goes = 128 * ((u // 8) % 4) + 12 * (u % 8) + 4 * g + u // 32
        perm[128 * g : 128 * g + 128] = jnp.where(goes == v, 1.0, 0.0).astype(BF16)

    def b_copy(dst):
        return pltpu.make_async_remote_copy(
            b_send.at[dst, 0:12], b_recv.at[rw, 0:12], ssem.at[3], rsem.at[3], device_id={"row": dst}, device_id_type=MESH
        )

    @pl.when(r_works)
    def _():
        a_recv[r] = a_send[rw]
        pltpu.make_async_copy(a_recv.at[0 : NROW - 1], a_recv.at[0 : NROW - 1], rsem.at[2]).wait()
        got = synthesize(fr_hi, fr_lo, a_recv[...].reshape(256, 128))
        b_send[...] = got.reshape(NROW, 16, 128)

        for step in ROW_STEPS:
            b_copy(row_step(step)).start()
        b_recv[rw] = b_send[r]
        pltpu.make_async_copy(b_recv.at[0 : RW - 1, 0:12], b_recv.at[0 : RW - 1, 0:12], rsem.at[3]).wait()

    @pl.when(jnp.logical_not(r_works))
    def _():
        pltpu.make_async_copy(b_recv.at[:, 0:12], b_recv.at[:, 0:12], rsem.at[3]).wait()

    x_hi, x_lo = split(b_recv[...].reshape(3, 144, 128))
    grid = None
    for g in range(3):
        p_g = perm[128 * g : 128 * g + 128]
        part = mm(x_hi[g], p_g) + mm(x_lo[g], p_g)
        grid = part if grid is None else grid + part
    ln = iota((16, 128), 1)
    for t in range(3):
        for n in range(4):
            z0, z1, z2 = (
                grid[48 * t + 16 * k : 48 * t + 16 * k + 16, 128 * n : 128 * n + 128] for k in range(3)
            )
            z1, z2 = pltpu.roll(z1, 96, 1), pltpu.roll(z2, 64, 1)
            o0 = jnp.where(ln < 96, z0, z1)
            o1 = jnp.where(ln < 64, z1, z2)
            rows = pl.ds(4 * t + n, 12, stride=12)
            oa[rows, :] = o0[0:12]
            ob[rows, :] = o1[0:12]
            oc[rows, :] = z2[0:12]
    out[:, 0:128] = oa[...]
    out[:, 128:256] = ob[...]
    out[:, 256:288] = oc[...][:, 0:32]

    @pl.when(z_works)
    def _():
        pltpu.make_async_copy(c_send.at[0 : ZW - 1], c_send.at[0 : ZW - 1], ssem.at[0]).wait()
        pltpu.make_async_copy(d_send.at[0 : NCOL - 1], d_send.at[0 : NCOL - 1], ssem.at[1]).wait()

    @pl.when(jnp.logical_not(z_works))
    def _():
        pltpu.make_async_copy(c_send, c_send, ssem.at[0]).wait()

    @pl.when(r_works)
    def _():
        pltpu.make_async_copy(a_send.at[0 : RW - 1], a_send.at[0 : RW - 1], ssem.at[2]).wait()
        pltpu.make_async_copy(b_send.at[0 : NROW - 1, 0:12], b_send.at[0 : NROW - 1, 0:12], ssem.at[3]).wait()

    @pl.when(jnp.logical_not(r_works))
    def _():
        pltpu.make_async_copy(a_send, a_send, ssem.at[2]).wait()


def on_device(covariance, coef_index):
    v = pltpu.VMEM
    return pl.pallas_call(
        kernel,
        out_shape=pltpu.VMEM((144, 288), F32),
        in_specs=[pl.BlockSpec(memory_space=pl.ANY)] * 2,
        out_specs=pl.BlockSpec(memory_space=pltpu.VMEM),
        scratch_shapes=[
            v((512, 1024), BF16),
            v((3, 16384), I32),
            v((64, 128), F32),
            v((LL, LANES), F32),
            v((LL, LANES), F32),
            v((LL, LANES), F32),
            v((LL, LANES), F32),
            v((NLON, 256), BF16),
            v((NLON, 256), BF16),
            v((512, 256), BF16),
            v((512, 256), BF16),
            v((384, 512), BF16),
            v((ZW, 16, 128), F32),
            v((NCOL, 16, 128), F32),
            v((NCOL, 24, 128), F32),
            v((ZW, 24, 128), F32),
            v((RW, 8, 128), F32),
            v((NROW, 8, 128), F32),
            v((NROW, 16, 128), F32),
            v((RW, 16, 128), F32),
            v((144, 128), F32),
            v((144, 128), F32),
            v((144, 128), F32),
            pltpu.SemaphoreType.DMA((2,)),
            pltpu.SemaphoreType.DMA((4,)),
            pltpu.SemaphoreType.DMA((4,)),
        ],
        compiler_params=pltpu.CompilerParams(collective_id=0, has_side_effects=True),
    )(covariance, coef_index)


def solution(mesh):
    return jax.shard_map(
        on_device,
        mesh=mesh,
        in_specs=(P("row", "col"), P()),
        out_specs=P("row", "col"),
        check_vma=False,
    )
```
